32 devices in a mesh: wide: 8 (over y, x, core), narrow: 4 (over z).
Axes of the slice: x: 2, y: 2, z: 4, core: 2. Of those that a mesh axis runs over, the one named last changes fastest.
Arguments:
- amplitudes: float32 [2, 8, 8, 4, 128, 128], P(None, None, 'wide', 'narrow'), may hold values from -6 to 6
- gates: float32 [3, 2, 2, 128, 128], replicated, may hold values from -0.375 to 0.375
Outputs:
- final_state: float32 [2, 8, 8, 4, 128, 128], P(None, None, 'wide', 'narrow')
The draws below stay inside these ranges and needn't reach their ends.
All inputs are finite; a program needn't handle non-finite values.
Results may differ from the reference program's by a relative error of at most 0.0001.
Values sent between devices are 32-bit elements; how exact they have to be, the bound alone decides.
A program may use at most 64 MiB of HBM per device.

```python
import jax
import jax.numpy as jnp
from jax import lax

ORDER = 128
SLABS = 8
N_WIDE = 8
N_NARROW = 4


def shard_levels(rng, dims, split, smallest, high):
    level = 1.0
    for dim, blocks in split:
        heights = jax.random.uniform(jax.random.fold_in(jax.random.fold_in(rng, 6), dim), (blocks,), jnp.float32, smallest / len(split), high / len(split))
        level = level * jnp.repeat(jnp.exp(heights), dims[dim] // blocks).reshape((-1,) + (1,) * (len(dims) - 1 - dim))
    return level


def scatter_about(key, dims, spread, most, split=(), dtype=jnp.bfloat16):
    gain = shard_levels(key, dims, split, -0.22, 0.18) if split else 1.0
    array = jax.random.normal(key, dims, jnp.float32) * spread * gain
    return jnp.minimum(jnp.maximum(array, -most), most).astype(dtype)


def setup_inputs(seed: int = 0) -> dict:
    key_list = jax.random.split(jax.random.key(seed), 3)
    amplitudes = scatter_about(key_list[0], (2, SLABS, N_WIDE, N_NARROW, ORDER, ORDER), 1.0, 6.0, ((2, 8), (3, 4)), jnp.float32)
    gates = scatter_about(key_list[1], (3, 2, 2, ORDER, ORDER), (2 * ORDER) ** -0.5, 0.375, (), jnp.float32)
    return {"amplitudes": amplitudes, "gates": gates}


def blocks(matrix):
    return jnp.stack([jnp.stack([matrix[0], -matrix[1]]), jnp.stack([matrix[1], matrix[0]])])


def on_rows(vector, matrix):
    return jnp.einsum("cdjk,drwnkb->crwnjb", blocks(matrix), vector, precision=lax.Precision.HIGHEST)


def on_columns(vector, matrix):
    return jnp.einsum("cdjk,drwnak->crwnaj", blocks(matrix), vector, precision=lax.Precision.HIGHEST)


def reference(amplitudes, gates):
    vector = amplitudes
    layout = amplitudes.shape
    for section_index in range(3):
        vector = on_rows(vector, gates[section_index, 0])
        vector = on_columns(vector, gates[section_index, 1])
        if section_index == 0:
            split_size = ORDER // N_WIDE
            vector = vector.reshape(2, SLABS, N_WIDE, N_NARROW, N_WIDE, split_size, ORDER)
            vector = vector.transpose(0, 1, 4, 3, 2, 5, 6).reshape(layout)
        if section_index == 1:
            split_size = ORDER // N_NARROW
            vector = vector.reshape(2, SLABS, N_WIDE, N_NARROW, N_NARROW, split_size, ORDER)
            vector = vector.transpose(0, 1, 2, 4, 3, 5, 6).reshape(layout)
    return vector
```

```python
import functools

import jax
import jax.numpy as jnp
from jax import lax
from jax.experimental import pallas as pl
from jax.experimental.pallas import tpu as pltpu
from jax.sharding import PartitionSpec as P

precise = lax.Precision.HIGHEST
MESH = pl.DeviceIdType.MESH
F32 = jnp.float32
BF16 = jnp.bfloat16


def blocks(matrix):
    return jnp.stack([jnp.stack([matrix[0], -matrix[1]]), jnp.stack([matrix[1], matrix[0]])])


def on_rows(vector, matrix):
    return jnp.einsum("cdjk,drkb->crjb", blocks(matrix), vector, precision=precise)


def on_columns(vector, matrix):
    return jnp.einsum("cdjk,drak->craj", blocks(matrix), vector, precision=precise)


def plain(amplitudes, gates):
    layout = amplitudes.shape
    slabs, order = layout[1], layout[4]
    vector = amplitudes.reshape(2, slabs, order, order)
    vector = on_columns(on_rows(vector, gates[0, 0]), gates[0, 1])
    vector = lax.all_to_all(vector.reshape(layout), "wide", split_axis=4, concat_axis=2, tiled=True)
    vector = vector.reshape(2, slabs, order, order)
    vector = on_columns(on_rows(vector, gates[1, 0]), gates[1, 1])
    vector = lax.all_to_all(vector.reshape(layout), "narrow", split_axis=4, concat_axis=3, tiled=True)
    vector = vector.reshape(2, slabs, order, order)
    vector = on_columns(on_rows(vector, gates[2, 0]), gates[2, 1])
    return vector.reshape(layout)


def partner(me, mask, count):
    out, bit = 0, 1
    while bit < count:
        digit = me // bit % 2
        if mask & bit:
            digit = 1 - digit
        out = out + digit * bit
        bit *= 2
    return out


def far_first(count):
    return sorted(range(1, count), key=lambda m: (-bin(m >> 1).count("1"), -m))


def split(value):
    high = value.astype(BF16)
    return high, (value - high.astype(F32)).astype(BF16)


def real_form(matrix):
    re, im = matrix[0], matrix[1]
    return jnp.concatenate(
        [jnp.concatenate([re, -im], axis=1), jnp.concatenate([im, re], axis=1)], axis=0
    )


def kernel(wide, narrow, amp, gates, out, x, g, y, yr, z, zr, left, right,
           load_sem, gate_sem, ws_sem, wr_sem, ns_sem, nr_sem):
    slabs, order = x.shape[1], x.shape[2]
    hw, hn = order // wide, order // narrow
    w, n = lax.axis_index("wide"), lax.axis_index("narrow")
    wide_masks = far_first(wide)
    narrow_masks = sorted(range(1, narrow), reverse=True)

    barrier = pltpu.get_barrier_semaphore()
    for mask in wide_masks:
        pl.semaphore_signal(barrier, inc=1, device_id=(partner(w, mask, wide), n), device_id_type=MESH)
    for mask in narrow_masks:
        pl.semaphore_signal(barrier, inc=1, device_id=(w, partner(n, mask, narrow)), device_id_type=MESH)

    def load(c):
        return pltpu.make_async_copy(amp.at[:, c], x.at[:, c], load_sem.at[c])

    def load_gate(t, k):
        return pltpu.make_async_copy(gates.at[t, k], g.at[t, k], gate_sem.at[t, k])

    load_gate(0, 0).start()
    load(0).start()
    for t in range(3):
        for k in range(2):
            if (t, k) != (0, 0):
                load_gate(t, k).start()
    for c in range(1, slabs):
        load(c).start()

    def send_wide(c, i):
        there = partner(w, wide_masks[i], wide)
        return pltpu.make_async_remote_copy(
            src_ref=y.at[c, :, pl.ds(pl.multiple_of(there * hw, hw), hw), :],
            dst_ref=yr.at[c, :, pl.ds(pl.multiple_of(w * hw, hw), hw), :],
            send_sem=ws_sem.at[c, i], recv_sem=wr_sem.at[c, i],
            device_id=(there, n), device_id_type=MESH)

    def send_narrow(c, i):
        there = partner(n, narrow_masks[i], narrow)
        return pltpu.make_async_remote_copy(
            src_ref=z.at[c, :, pl.ds(pl.multiple_of(there * hn, hn), hn), :],
            dst_ref=zr.at[c, :, pl.ds(pl.multiple_of(n * hn, hn), hn), :],
            send_sem=ns_sem.at[c, i], recv_sem=nr_sem.at[c, i],
            device_id=(w, there), device_id_type=MESH)

    def prepare(t):
        load_gate(t, 0).wait()
        high, low = split(real_form(g[t, 0]))
        left[t] = jnp.concatenate([high, low, high], axis=1)

    def rows(t, value):
        high, low = split(value.reshape(2 * order, order))
        stacked = jnp.concatenate([high, high, low], axis=0)
        return jnp.dot(left[t], stacked, preferred_element_type=F32)

    def columns(value):
        high, low = split(jnp.concatenate([value[:order], value[order:]], axis=1))
        stacked = jnp.concatenate([high, low, high], axis=1)
        return jnp.dot(stacked, right[...], preferred_element_type=F32)

    def first(c):
        load(c).wait()
        y[c] = rows(0, x[:, c]).reshape(2, order, order)

    def start_wide(c):
        for i in range(wide - 1):
            send_wide(c, i).start()

    prepare(0)
    first(0)
    pl.semaphore_wait(barrier, wide + narrow - 2)
    start_wide(0)

    @pl.loop(1, slabs)
    def _(c):
        first(c)
        start_wide(c)

    prepare(1)
    for t in range(3):
        load_gate(t, 1).wait()
    product = g[0, 1].reshape(2 * order, order)
    for t in (1, 2):
        product = jnp.dot(real_form(g[t, 1]), product, precision=precise, preferred_element_type=F32)
    re, im = product[:order].T, product[order:].T
    high, low = split(jnp.concatenate(
        [jnp.concatenate([re, im], axis=1), jnp.concatenate([-im, re], axis=1)], axis=0))
    right[...] = jnp.concatenate([high, high, low], axis=0)
    prepare(2)

    def second(c, with_columns):
        own = pl.ds(pl.multiple_of(w * hw, hw), hw)
        yr[c, :, own, :] = y[c, :, own, :]
        for i in range(wide - 1):
            send_wide(c, i).wait_recv()
        value = rows(1, yr[c])
        if with_columns:
            value = columns(value)
            z[c, 0] = value[:, :order]
            z[c, 1] = value[:, order:]
        else:
            z[c] = value.reshape(2, order, order)
        for i in range(narrow - 1):
            send_narrow(c, i).start()

    second(0, False)

    @pl.loop(1, slabs)
    def _(c):
        second(c, True)

    def third(c, with_columns):
        own = pl.ds(pl.multiple_of(n * hn, hn), hn)
        zr[c, :, own, :] = z[c, :, own, :]
        for i in range(narrow - 1):
            send_narrow(c, i).wait_recv()
        value = rows(2, zr[c])
        if with_columns:
            value = columns(value)
            out[0, c] = value[:, :order]
            out[1, c] = value[:, order:]
        else:
            out[0, c] = value[:order]
            out[1, c] = value[order:]

    third(0, True)

    @pl.loop(1, slabs)
    def _(c):
        third(c, False)

    @pl.loop(0, slabs)
    def _(c):
        for i in range(wide - 1):
            send_wide(c, i).wait_send()
        for i in range(narrow - 1):
            send_narrow(c, i).wait_send()


def fused(wide, narrow, amplitudes, gates):
    layout = amplitudes.shape
    slabs, order = layout[1], layout[4]
    vector = amplitudes.reshape(2, slabs, order, order)
    slab_buffer = pltpu.VMEM((slabs, 2, order, order), F32)
    result = pl.pallas_call(
        functools.partial(kernel, wide, narrow),
        out_shape=jax.ShapeDtypeStruct(vector.shape, F32),
        in_specs=[pl.BlockSpec(memory_space=pl.ANY)] * 2,
        out_specs=pl.BlockSpec(memory_space=pltpu.VMEM),
        scratch_shapes=[
            pltpu.VMEM(vector.shape, F32),
            pltpu.VMEM(gates.shape, F32),
            slab_buffer, slab_buffer, slab_buffer, slab_buffer,
            pltpu.VMEM((3, 2 * order, 6 * order), BF16),
            pltpu.VMEM((6 * order, 2 * order), BF16),
            pltpu.SemaphoreType.DMA((slabs,)),
            pltpu.SemaphoreType.DMA((3, 2)),
            pltpu.SemaphoreType.DMA((slabs, wide - 1)),
            pltpu.SemaphoreType.DMA((slabs, wide - 1)),
            pltpu.SemaphoreType.DMA((slabs, narrow - 1)),
            pltpu.SemaphoreType.DMA((slabs, narrow - 1)),
        ],
        compiler_params=pltpu.CompilerParams(
            collective_id=0, has_side_effects=True, vmem_limit_bytes=24 << 20),
    )(vector, gates)
    return result.reshape(layout)


def tiled(order, count):
    return count > 1 and count & (count - 1) == 0 and order % (8 * count) == 0


def solution(mesh):
    wide, narrow = mesh.shape["wide"], mesh.shape["narrow"]

    def shards(amplitudes, gates):
        order = amplitudes.shape[4]
        if tiled(order, wide) and tiled(order, narrow) and wide * narrow <= 128:
            return fused(wide, narrow, amplitudes, gates)
        return plain(amplitudes, gates)

    return jax.shard_map(
        shards,
        mesh=mesh,
        in_specs=(P(None, None, "wide", "narrow", None, None), P()),
        out_specs=P(None, None, "wide", "narrow", None, None),
        check_vma=False,
    )
```

```python
import functools

import jax
import jax.numpy as jnp
from jax import lax
from jax.experimental import pallas as pl
from jax.experimental.pallas import tpu as pltpu
from jax.sharding import PartitionSpec as P

precise = lax.Precision.HIGHEST
MESH = pl.DeviceIdType.MESH
F32 = jnp.float32
BF16 = jnp.bfloat16


def blocks(matrix):
    return jnp.stack([jnp.stack([matrix[0], -matrix[1]]), jnp.stack([matrix[1], matrix[0]])])


def on_rows(vector, matrix):
    return jnp.einsum("cdjk,drkb->crjb", blocks(matrix), vector, precision=precise)


def on_columns(vector, matrix):
    return jnp.einsum("cdjk,drak->craj", blocks(matrix), vector, precision=precise)


def plain(amplitudes, gates):
    layout = amplitudes.shape
    slabs, order = layout[1], layout[4]
    vector = amplitudes.reshape(2, slabs, order, order)
    vector = on_columns(on_rows(vector, gates[0, 0]), gates[0, 1])
    vector = lax.all_to_all(vector.reshape(layout), "wide", split_axis=4, concat_axis=2, tiled=True)
    vector = vector.reshape(2, slabs, order, order)
    vector = on_columns(on_rows(vector, gates[1, 0]), gates[1, 1])
    vector = lax.all_to_all(vector.reshape(layout), "narrow", split_axis=4, concat_axis=3, tiled=True)
    vector = vector.reshape(2, slabs, order, order)
    vector = on_columns(on_rows(vector, gates[2, 0]), gates[2, 1])
    return vector.reshape(layout)


def partner(me, mask, count):
    out, bit = 0, 1
    while bit < count:
        digit = me // bit % 2
        if mask & bit:
            digit = 1 - digit
        out = out + digit * bit
        bit *= 2
    return out


def far_first(count):
    return sorted(range(1, count), key=lambda m: (-bin(m >> 1).count("1"), -m))


def split(value):
    high = value.astype(BF16)
    return high, (value - high.astype(F32)).astype(BF16)


def real_form(matrix):
    re, im = matrix[0], matrix[1]
    return jnp.concatenate(
        [jnp.concatenate([re, -im], axis=1), jnp.concatenate([im, re], axis=1)], axis=0
    )


def kernel(wide, narrow, amp, gates, out, x, g, y, yr, z, zr, left, right,
           load_sem, gate_sem, ws_sem, wr_sem, ns_sem, nr_sem):
    slabs, order = x.shape[1], x.shape[2]
    hw, hn = order // wide, order // narrow
    w, n = lax.axis_index("wide"), lax.axis_index("narrow")
    wide_masks = far_first(wide)
    narrow_masks = sorted(range(1, narrow), reverse=True)

    barrier = pltpu.get_barrier_semaphore()
    for mask in wide_masks:
        pl.semaphore_signal(barrier, inc=1, device_id=(partner(w, mask, wide), n), device_id_type=MESH)
    for mask in narrow_masks:
        pl.semaphore_signal(barrier, inc=1, device_id=(w, partner(n, mask, narrow)), device_id_type=MESH)

    def load(c):
        return pltpu.make_async_copy(amp.at[:, c], x.at[:, c], load_sem.at[c])

    def load_gate(t, k):
        return pltpu.make_async_copy(gates.at[t, k], g.at[t, k], gate_sem.at[t, k])

    load_gate(0, 0).start()
    load(0).start()
    for t in range(3):
        for k in range(2):
            if (t, k) != (0, 0):
                load_gate(t, k).start()
    for c in range(1, slabs):
        load(c).start()

    def send_wide(c, i):
        there = partner(w, wide_masks[i], wide)
        return pltpu.make_async_remote_copy(
            src_ref=y.at[c, :, pl.ds(pl.multiple_of(there * hw, hw), hw), :],
            dst_ref=yr.at[c, :, pl.ds(pl.multiple_of(w * hw, hw), hw), :],
            send_sem=ws_sem.at[c, i], recv_sem=wr_sem.at[c, i],
            device_id=(there, n), device_id_type=MESH)

    def send_narrow(c, i):
        there = partner(n, narrow_masks[i], narrow)
        return pltpu.make_async_remote_copy(
            src_ref=z.at[c, :, pl.ds(pl.multiple_of(there * hn, hn), hn), :],
            dst_ref=zr.at[c, :, pl.ds(pl.multiple_of(n * hn, hn), hn), :],
            send_sem=ns_sem.at[c, i], recv_sem=nr_sem.at[c, i],
            device_id=(w, there), device_id_type=MESH)

    def prepare(t):
        load_gate(t, 0).wait()
        high, low = split(real_form(g[t, 0]))
        left[t] = jnp.concatenate([high, low, high], axis=1)

    def rows(t, value):
        high, low = split(value.reshape(2 * order, order))
        stacked = jnp.concatenate([high, high, low], axis=0)
        return jnp.dot(left[t], stacked, preferred_element_type=F32)

    def columns(value):
        high, low = split(jnp.concatenate([value[:order], value[order:]], axis=1))
        stacked = jnp.concatenate([high, low, high], axis=1)
        return jnp.dot(stacked, right[...], preferred_element_type=F32)

    def first(c):
        load(c).wait()
        y[c] = rows(0, x[:, c]).reshape(2, order, order)

    def start_wide(c):
        for i in range(wide - 1):
            send_wide(c, i).start()

    prepare(0)
    first(0)
    pl.semaphore_wait(barrier, wide + narrow - 2)
    start_wide(0)
    prepare(1)

    @pl.loop(1, slabs)
    def _(c):
        first(c)
        start_wide(c)

    def second(c, with_columns):
        own = pl.ds(pl.multiple_of(w * hw, hw), hw)
        yr[c, :, own, :] = y[c, :, own, :]
        for i in range(wide - 1):
            send_wide(c, i).wait_recv()
        value = rows(1, yr[c])
        if with_columns:
            value = columns(value)
            z[c, 0] = value[:, :order]
            z[c, 1] = value[:, order:]
        else:
            z[c] = value.reshape(2, order, order)
        for i in range(narrow - 1):
            send_narrow(c, i).start()

    second(0, False)

    for t in range(3):
        load_gate(t, 1).wait()
    product = g[0, 1].reshape(2 * order, order)
    for t in (1, 2):
        product = jnp.dot(real_form(g[t, 1]), product, precision=precise, preferred_element_type=F32)
    re, im = product[:order].T, product[order:].T
    high, low = split(jnp.concatenate(
        [jnp.concatenate([re, im], axis=1), jnp.concatenate([-im, re], axis=1)], axis=0))
    right[...] = jnp.concatenate([high, high, low], axis=0)
    prepare(2)

    @pl.loop(1, slabs)
    def _(c):
        second(c, True)

    def third(c, with_columns):
        own = pl.ds(pl.multiple_of(n * hn, hn), hn)
        zr[c, :, own, :] = z[c, :, own, :]
        for i in range(narrow - 1):
            send_narrow(c, i).wait_recv()
        value = rows(2, zr[c])
        if with_columns:
            value = columns(value)
            out[0, c] = value[:, :order]
            out[1, c] = value[:, order:]
        else:
            out[0, c] = value[:order]
            out[1, c] = value[order:]

    third(0, True)

    @pl.loop(1, slabs)
    def _(c):
        third(c, False)

    @pl.loop(0, slabs)
    def _(c):
        for i in range(wide - 1):
            send_wide(c, i).wait_send()
        for i in range(narrow - 1):
            send_narrow(c, i).wait_send()


def fused(wide, narrow, amplitudes, gates):
    layout = amplitudes.shape
    slabs, order = layout[1], layout[4]
    vector = amplitudes.reshape(2, slabs, order, order)
    slab_buffer = pltpu.VMEM((slabs, 2, order, order), F32)
    result = pl.pallas_call(
        functools.partial(kernel, wide, narrow),
        out_shape=jax.ShapeDtypeStruct(vector.shape, F32),
        in_specs=[pl.BlockSpec(memory_space=pl.ANY)] * 2,
        out_specs=pl.BlockSpec(memory_space=pltpu.VMEM),
        scratch_shapes=[
            pltpu.VMEM(vector.shape, F32),
            pltpu.VMEM(gates.shape, F32),
            slab_buffer, slab_buffer, slab_buffer, slab_buffer,
            pltpu.VMEM((3, 2 * order, 6 * order), BF16),
            pltpu.VMEM((6 * order, 2 * order), BF16),
            pltpu.SemaphoreType.DMA((slabs,)),
            pltpu.SemaphoreType.DMA((3, 2)),
            pltpu.SemaphoreType.DMA((slabs, wide - 1)),
            pltpu.SemaphoreType.DMA((slabs, wide - 1)),
            pltpu.SemaphoreType.DMA((slabs, narrow - 1)),
            pltpu.SemaphoreType.DMA((slabs, narrow - 1)),
        ],
        compiler_params=pltpu.CompilerParams(
            collective_id=0, has_side_effects=True, vmem_limit_bytes=24 << 20),
    )(*[pltpu.with_memory_space_constraint(value, pltpu.HBM) for value in (vector, gates)])
    return result.reshape(layout)


def tiled(order, count):
    return count > 1 and count & (count - 1) == 0 and order % (8 * count) == 0


def solution(mesh):
    wide, narrow = mesh.shape["wide"], mesh.shape["narrow"]

    def shards(amplitudes, gates):
        order = amplitudes.shape[4]
        if tiled(order, wide) and tiled(order, narrow) and wide * narrow <= 128:
            return fused(wide, narrow, amplitudes, gates)
        return plain(amplitudes, gates)

    return jax.shard_map(
        shards,
        mesh=mesh,
        in_specs=(P(None, None, "wide", "narrow", None, None), P()),
        out_specs=P(None, None, "wide", "narrow", None, None),
        check_vma=False,
    )
```

```python
import functools

import jax
import jax.numpy as jnp
from jax import lax
from jax.experimental import pallas as pl
from jax.experimental.pallas import tpu as pltpu
from jax.sharding import PartitionSpec as P

precise = lax.Precision.HIGHEST
MESH = pl.DeviceIdType.MESH
F32 = jnp.float32
BF16 = jnp.bfloat16


def blocks(matrix):
    return jnp.stack([jnp.stack([matrix[0], -matrix[1]]), jnp.stack([matrix[1], matrix[0]])])


def on_rows(vector, matrix):
    return jnp.einsum("cdjk,drkb->crjb", blocks(matrix), vector, precision=precise)


def on_columns(vector, matrix):
    return jnp.einsum("cdjk,drak->craj", blocks(matrix), vector, precision=precise)


def plain(amplitudes, gates):
    layout = amplitudes.shape
    slabs, order = layout[1], layout[4]
    vector = amplitudes.reshape(2, slabs, order, order)
    vector = on_columns(on_rows(vector, gates[0, 0]), gates[0, 1])
    vector = lax.all_to_all(vector.reshape(layout), "wide", split_axis=4, concat_axis=2, tiled=True)
    vector = vector.reshape(2, slabs, order, order)
    vector = on_columns(on_rows(vector, gates[1, 0]), gates[1, 1])
    vector = lax.all_to_all(vector.reshape(layout), "narrow", split_axis=4, concat_axis=3, tiled=True)
    vector = vector.reshape(2, slabs, order, order)
    vector = on_columns(on_rows(vector, gates[2, 0]), gates[2, 1])
    return vector.reshape(layout)


def partner(me, mask, count):
    out, bit = 0, 1
    while bit < count:
        digit = me // bit % 2
        if mask & bit:
            digit = 1 - digit
        out = out + digit * bit
        bit *= 2
    return out


def far_first(count):
    return sorted(range(1, count), key=lambda m: (-bin(m >> 1).count("1"), -m))


def split(value):
    high = value.astype(BF16)
    return high, (value - high.astype(F32)).astype(BF16)


def real_form(matrix):
    re, im = matrix[0], matrix[1]
    return jnp.concatenate(
        [jnp.concatenate([re, -im], axis=1), jnp.concatenate([im, re], axis=1)], axis=0
    )


def kernel(wide, narrow, amp, gates, out, x, g, y, yr, z, zr, left, right,
           load_sem, gate_sem, ws_sem, wr_sem, ns_sem, nr_sem, ready_sem):
    slabs, order = x.shape[1], x.shape[2]
    hw, hn = order // wide, order // narrow
    w, n = lax.axis_index("wide"), lax.axis_index("narrow")
    wide_masks = far_first(wide)
    narrow_masks = sorted(range(1, narrow), reverse=True)

    barrier = pltpu.get_barrier_semaphore()
    for mask in wide_masks:
        pl.semaphore_signal(barrier, inc=1, device_id=(partner(w, mask, wide), n), device_id_type=MESH)
    relay = narrow == 4
    inner = n * (3 - n) // 2
    for mask in narrow_masks:
        def greet(mask=mask):
            pl.semaphore_signal(
                barrier, inc=1, device_id=(w, partner(n, mask, narrow)), device_id_type=MESH)
        if relay and mask == 3:
            pl.when(inner == 1)(greet)
        else:
            greet()
    greetings = wide + narrow - 2 + (inner - 1 if relay else 0)

    def load(c):
        return pltpu.make_async_copy(amp.at[:, c], x.at[:, c], load_sem.at[c])

    def load_gate(t, k):
        return pltpu.make_async_copy(gates.at[t, k], g.at[t, k], gate_sem.at[t, k])

    load_gate(0, 0).start()
    load(0).start()
    for t in range(3):
        for k in range(2):
            if (t, k) != (0, 0):
                load_gate(t, k).start()
    for c in range(1, slabs):
        load(c).start()

    def send_wide(c, i):
        there = partner(w, wide_masks[i], wide)
        return pltpu.make_async_remote_copy(
            src_ref=y.at[c, :, pl.ds(pl.multiple_of(there * hw, hw), hw), :],
            dst_ref=yr.at[c, :, pl.ds(pl.multiple_of(w * hw, hw), hw), :],
            send_sem=ws_sem.at[c, i], recv_sem=wr_sem.at[c, i],
            device_id=(there, n), device_id_type=MESH)

    def send_narrow(c, i):
        there = partner(n, narrow_masks[i], narrow)
        return pltpu.make_async_remote_copy(
            src_ref=z.at[c, :, pl.ds(pl.multiple_of(there * hn, hn), hn), :],
            dst_ref=zr.at[c, :, pl.ds(pl.multiple_of(n * hn, hn), hn), :],
            send_sem=ns_sem.at[c, i], recv_sem=nr_sem.at[c, i],
            device_id=(w, there), device_id_type=MESH)

    def prepare(t):
        load_gate(t, 0).wait()
        high, low = split(real_form(g[t, 0]))
        left[t] = jnp.concatenate([high, low, high], axis=1)

    def rows(t, value):
        high, low = split(value.reshape(2 * order, order))
        stacked = jnp.concatenate([high, high, low], axis=0)
        return jnp.dot(left[t], stacked, preferred_element_type=F32)

    def columns(value):
        high, low = split(jnp.concatenate([value[:order], value[order:]], axis=1))
        stacked = jnp.concatenate([high, low, high], axis=1)
        return jnp.dot(stacked, right[...], preferred_element_type=F32)

    def first(c):
        load(c).wait()
        y[c] = rows(0, x[:, c]).reshape(2, order, order)

    def start_wide(c):
        for i in range(wide - 1):
            send_wide(c, i).start()

    prepare(0)
    first(0)
    pl.semaphore_wait(barrier, greetings)
    start_wide(0)
    if relay:
        pl.semaphore_signal(
            ready_sem, inc=1, device_id=(w, partner(n, 1, narrow)), device_id_type=MESH)
    prepare(1)

    @pl.loop(1, slabs)
    def _(c):
        first(c)
        start_wide(c)

    def second(c, with_columns):
        own = pl.ds(pl.multiple_of(w * hw, hw), hw)
        yr[c, :, own, :] = y[c, :, own, :]
        for i in range(wide - 1):
            send_wide(c, i).wait_recv()
        value = rows(1, yr[c])
        if with_columns:
            value = columns(value)
            z[c, 0] = value[:, :order]
            z[c, 1] = value[:, order:]
        else:
            z[c] = value.reshape(2, order, order)
        for i in range(narrow - 1):
            send_narrow(c, i).start()

    if relay:
        pl.semaphore_wait(ready_sem, 1)
    second(0, False)

    for t in range(3):
        load_gate(t, 1).wait()
    product = g[0, 1].reshape(2 * order, order)
    for t in (1, 2):
        product = jnp.dot(real_form(g[t, 1]), product, precision=precise, preferred_element_type=F32)
    re, im = product[:order].T, product[order:].T
    high, low = split(jnp.concatenate(
        [jnp.concatenate([re, im], axis=1), jnp.concatenate([-im, re], axis=1)], axis=0))
    right[...] = jnp.concatenate([high, high, low], axis=0)
    prepare(2)

    @pl.loop(1, slabs)
    def _(c):
        second(c, True)

    def third(c, with_columns):
        own = pl.ds(pl.multiple_of(n * hn, hn), hn)
        zr[c, :, own, :] = z[c, :, own, :]
        for i in range(narrow - 1):
            send_narrow(c, i).wait_recv()
        value = rows(2, zr[c])
        if with_columns:
            value = columns(value)
            out[0, c] = value[:, :order]
            out[1, c] = value[:, order:]
        else:
            out[0, c] = value[:order]
            out[1, c] = value[order:]

    third(0, True)

    @pl.loop(1, slabs)
    def _(c):
        third(c, False)

    @pl.loop(0, slabs)
    def _(c):
        for i in range(wide - 1):
            send_wide(c, i).wait_send()
        for i in range(narrow - 1):
            send_narrow(c, i).wait_send()


def fused(wide, narrow, amplitudes, gates):
    layout = amplitudes.shape
    slabs, order = layout[1], layout[4]
    vector = amplitudes.reshape(2, slabs, order, order)
    slab_buffer = pltpu.VMEM((slabs, 2, order, order), F32)
    result = pl.pallas_call(
        functools.partial(kernel, wide, narrow),
        out_shape=jax.ShapeDtypeStruct(vector.shape, F32),
        in_specs=[pl.BlockSpec(memory_space=pl.ANY)] * 2,
        out_specs=pl.BlockSpec(memory_space=pltpu.VMEM),
        scratch_shapes=[
            pltpu.VMEM(vector.shape, F32),
            pltpu.VMEM(gates.shape, F32),
            slab_buffer, slab_buffer, slab_buffer, slab_buffer,
            pltpu.VMEM((3, 2 * order, 6 * order), BF16),
            pltpu.VMEM((6 * order, 2 * order), BF16),
            pltpu.SemaphoreType.DMA((slabs,)),
            pltpu.SemaphoreType.DMA((3, 2)),
            pltpu.SemaphoreType.DMA((slabs, wide - 1)),
            pltpu.SemaphoreType.DMA((slabs, wide - 1)),
            pltpu.SemaphoreType.DMA((slabs, narrow - 1)),
            pltpu.SemaphoreType.DMA((slabs, narrow - 1)),
            pltpu.SemaphoreType.REGULAR,
        ],
        compiler_params=pltpu.CompilerParams(
            collective_id=0, has_side_effects=True, vmem_limit_bytes=24 << 20),
    )(*[pltpu.with_memory_space_constraint(value, pltpu.HBM) for value in (vector, gates)])
    return result.reshape(layout)


def tiled(order, count):
    return count > 1 and count & (count - 1) == 0 and order % (8 * count) == 0


def solution(mesh):
    wide, narrow = mesh.shape["wide"], mesh.shape["narrow"]

    def shards(amplitudes, gates):
        order = amplitudes.shape[4]
        if tiled(order, wide) and tiled(order, narrow) and wide * narrow <= 128:
            return fused(wide, narrow, amplitudes, gates)
        return plain(amplitudes, gates)

    return jax.shard_map(
        shards,
        mesh=mesh,
        in_specs=(P(None, None, "wide", "narrow", None, None), P()),
        out_specs=P(None, None, "wide", "narrow", None, None),
        check_vma=False,
    )
```

```python
import functools

import jax
import jax.numpy as jnp
from jax import lax
from jax.experimental import pallas as pl
from jax.experimental.pallas import tpu as pltpu
from jax.sharding import PartitionSpec as P

precise = lax.Precision.HIGHEST
MESH = pl.DeviceIdType.MESH
F32 = jnp.float32
BF16 = jnp.bfloat16
EARLY_AT = 4
TAIL = 1


def blocks(matrix):
    return jnp.stack([jnp.stack([matrix[0], -matrix[1]]), jnp.stack([matrix[1], matrix[0]])])


def on_rows(vector, matrix):
    return jnp.einsum("cdjk,drkb->crjb", blocks(matrix), vector, precision=precise)


def on_columns(vector, matrix):
    return jnp.einsum("cdjk,drak->craj", blocks(matrix), vector, precision=precise)


def plain(amplitudes, gates):
    layout = amplitudes.shape
    slabs, order = layout[1], layout[4]
    vector = amplitudes.reshape(2, slabs, order, order)
    vector = on_columns(on_rows(vector, gates[0, 0]), gates[0, 1])
    vector = lax.all_to_all(vector.reshape(layout), "wide", split_axis=4, concat_axis=2, tiled=True)
    vector = vector.reshape(2, slabs, order, order)
    vector = on_columns(on_rows(vector, gates[1, 0]), gates[1, 1])
    vector = lax.all_to_all(vector.reshape(layout), "narrow", split_axis=4, concat_axis=3, tiled=True)
    vector = vector.reshape(2, slabs, order, order)
    vector = on_columns(on_rows(vector, gates[2, 0]), gates[2, 1])
    return vector.reshape(layout)


def partner(me, mask, count):
    out, bit = 0, 1
    while bit < count:
        digit = me // bit % 2
        if mask & bit:
            digit = 1 - digit
        out = out + digit * bit
        bit *= 2
    return out


def far_first(count):
    return sorted(range(1, count), key=lambda m: (-bin(m >> 1).count("1"), -m))


def split(value):
    high = value.astype(BF16)
    return high, (value - high.astype(F32)).astype(BF16)


def real_form(matrix):
    re, im = matrix[0], matrix[1]
    return jnp.concatenate(
        [jnp.concatenate([re, -im], axis=1), jnp.concatenate([im, re], axis=1)], axis=0
    )


def kernel(wide, narrow, early, amp, gates, out, x, g, y, yr, z, zr, left, right,
           load_sem, gate_sem, ws_sem, wr_sem, ns_sem, nr_sem, es_sem, er_sem):
    slabs, order = amp.shape[1], amp.shape[2]
    last = slabs - 1
    hw, hn = order // wide, order // narrow
    w, n = lax.axis_index("wide"), lax.axis_index("narrow")
    wide_masks = far_first(wide)
    narrow_masks = sorted(range(1, narrow), reverse=True)

    barrier = pltpu.get_barrier_semaphore()
    for mask in wide_masks:
        pl.semaphore_signal(barrier, inc=1, device_id=(partner(w, mask, wide), n), device_id_type=MESH)
    for mask in narrow_masks:
        pl.semaphore_signal(barrier, inc=1, device_id=(w, partner(n, mask, narrow)), device_id_type=MESH)

    def load(c):
        return pltpu.make_async_copy(amp.at[:, c], x.at[:, c], load_sem.at[c])

    def load_gate(t, k):
        return pltpu.make_async_copy(gates.at[t, k], g.at[t, k], gate_sem.at[t, k])

    load_gate(0, 0).start()
    if early:
        load(last).start()
    load(0).start()
    for t in range(3):
        for k in range(2):
            if (t, k) != (0, 0):
                load_gate(t, k).start()
    for c in range(1, last if early else slabs):
        load(c).start()

    def send_wide(c, i):
        there = partner(w, wide_masks[i], wide)
        return pltpu.make_async_remote_copy(
            src_ref=y.at[c, :, pl.ds(pl.multiple_of(there * hw, hw), hw), :],
            dst_ref=yr.at[c, :, pl.ds(pl.multiple_of(w * hw, hw), hw), :],
            send_sem=ws_sem.at[c, i], recv_sem=wr_sem.at[c, i],
            device_id=(there, n), device_id_type=MESH)

    def send_narrow(c, i):
        there = partner(n, narrow_masks[i], narrow)
        return pltpu.make_async_remote_copy(
            src_ref=z.at[c, :, pl.ds(pl.multiple_of(there * hn, hn), hn), :],
            dst_ref=zr.at[c, :, pl.ds(pl.multiple_of(n * hn, hn), hn), :],
            send_sem=ns_sem.at[c, i], recv_sem=nr_sem.at[c, i],
            device_id=(w, there), device_id_type=MESH)

    def send_early():
        return pltpu.make_async_remote_copy(
            src_ref=x.at[:, last], dst_ref=x.at[:, slabs],
            send_sem=es_sem.at[0], recv_sem=er_sem.at[0],
            device_id=(w, partner(n, 2, narrow)), device_id_type=MESH)

    def send_half(k):
        there = partner(n, 1, narrow)
        index = partner(n, 2 * k, narrow)
        return pltpu.make_async_remote_copy(
            src_ref=z.at[last + k, :, pl.ds(pl.multiple_of(there * hn, hn), hn), :],
            dst_ref=zr.at[last, :, pl.ds(pl.multiple_of(index * hn, hn), hn), :],
            send_sem=es_sem.at[1 + k], recv_sem=er_sem.at[1 + k],
            device_id=(w, there), device_id_type=MESH)

    def prepare(t):
        load_gate(t, 0).wait()
        high, low = split(real_form(g[t, 0]))
        left[t] = jnp.concatenate([high, low, high], axis=1)

    def rows(t, value):
        high, low = split(value.reshape(2 * order, order))
        stacked = jnp.concatenate([high, high, low], axis=0)
        return jnp.dot(left[t], stacked, preferred_element_type=F32)

    def columns(value):
        high, low = split(jnp.concatenate([value[:order], value[order:]], axis=1))
        stacked = jnp.concatenate([high, low, high], axis=1)
        return jnp.dot(stacked, right[...], preferred_element_type=F32)

    def first(c, loaded=False):
        if not loaded:
            load(c).wait()
        y[c] = rows(0, x[:, c]).reshape(2, order, order)

    def start_wide(c):
        for i in range(wide - 1):
            send_wide(c, i).start()

    prepare(0)
    first(0)
    if early:
        load(last).wait()
    pl.semaphore_wait(barrier, wide + narrow - 2)
    if early:
        send_early().start()
    start_wide(0)
    prepare(1)

    @pl.loop(1, last if early else slabs)
    def _(c):
        first(c)
        start_wide(c)

    if early:
        first(last, True)
        start_wide(last)

    def second(c, with_columns, with_narrow=True):
        own = pl.ds(pl.multiple_of(w * hw, hw), hw)
        yr[c, :, own, :] = y[c, :, own, :]
        for i in range(wide - 1):
            send_wide(c, i).wait_recv()
        value = rows(1, yr[c])
        if with_columns:
            value = columns(value)
            z[c, 0] = value[:, :order]
            z[c, 1] = value[:, order:]
        else:
            z[c] = value.reshape(2, order, order)
        if not with_narrow:
            return
        for i in range(narrow - 1):
            send_narrow(c, i).start()

    second(0, False)

    for t in range(3):
        load_gate(t, 1).wait()
    product = g[0, 1].reshape(2 * order, order)
    for t in (1, 2):
        product = jnp.dot(real_form(g[t, 1]), product, precision=precise, preferred_element_type=F32)
    re, im = product[:order].T, product[order:].T
    high, low = split(jnp.concatenate(
        [jnp.concatenate([re, im], axis=1), jnp.concatenate([-im, re], axis=1)], axis=0))
    right[...] = jnp.concatenate([high, high, low], axis=0)
    prepare(2)

    if early:
        @pl.loop(1, EARLY_AT)
        def _(c):
            second(c, True)

        send_early().wait_recv()
        first(slabs, True)
        start_wide(slabs)

        @pl.loop(EARLY_AT, last - TAIL)
        def _(c):
            second(c, True)

        @pl.loop(last, slabs + 1)
        def _(c):
            second(c, False, False)

        for k in range(2):
            send_half(k).start()
            index = partner(n, 2 * k, narrow)
            rows_to = pl.ds(pl.multiple_of(index * hn, hn), hn)
            rows_from = pl.ds(pl.multiple_of(n * hn, hn), hn)
            zr[last, :, rows_to, :] = z[last + k, :, rows_from, :]

        @pl.loop(last - TAIL, last)
        def _(c):
            second(c, True)
    else:
        @pl.loop(1, slabs)
        def _(c):
            second(c, True)

    def third(c, with_columns, exchanged=False):
        if not exchanged:
            own = pl.ds(pl.multiple_of(n * hn, hn), hn)
            zr[c, :, own, :] = z[c, :, own, :]
            for i in range(narrow - 1):
                send_narrow(c, i).wait_recv()
        value = rows(2, zr[c])
        if with_columns:
            value = columns(value)
            out[0, c] = value[:, :order]
            out[1, c] = value[:, order:]
        else:
            out[0, c] = value[:order]
            out[1, c] = value[order:]

    third(0, True)
    if early:
        @pl.loop(1, last - TAIL)
        def _(c):
            third(c, False)

        for k in range(2):
            send_half(k).wait_recv()
        third(last, True, True)

        @pl.loop(last - TAIL, last)
        def _(c):
            third(c, False)
    else:
        @pl.loop(1, slabs)
        def _(c):
            third(c, False)

    @pl.loop(0, slabs + 1 if early else slabs)
    def _(c):
        for i in range(wide - 1):
            send_wide(c, i).wait_send()

    @pl.loop(0, last if early else slabs)
    def _(c):
        for i in range(narrow - 1):
            send_narrow(c, i).wait_send()

    if early:
        send_early().wait_send()
        for k in range(2):
            send_half(k).wait_send()


def fused(wide, narrow, amplitudes, gates):
    layout = amplitudes.shape
    slabs, order = layout[1], layout[4]
    vector = amplitudes.reshape(2, slabs, order, order)
    early = narrow == 4 and slabs > EARLY_AT + TAIL
    slots = slabs + early
    slab_buffer = pltpu.VMEM((slots, 2, order, order), F32)
    result = pl.pallas_call(
        functools.partial(kernel, wide, narrow, early),
        out_shape=jax.ShapeDtypeStruct(vector.shape, F32),
        in_specs=[pl.BlockSpec(memory_space=pl.ANY)] * 2,
        out_specs=pl.BlockSpec(memory_space=pltpu.VMEM),
        scratch_shapes=[
            pltpu.VMEM((2, slots, order, order), F32),
            pltpu.VMEM(gates.shape, F32),
            slab_buffer, slab_buffer, slab_buffer, slab_buffer,
            pltpu.VMEM((3, 2 * order, 6 * order), BF16),
            pltpu.VMEM((6 * order, 2 * order), BF16),
            pltpu.SemaphoreType.DMA((slabs,)),
            pltpu.SemaphoreType.DMA((3, 2)),
            pltpu.SemaphoreType.DMA((slots, wide - 1)),
            pltpu.SemaphoreType.DMA((slots, wide - 1)),
            pltpu.SemaphoreType.DMA((slabs, narrow - 1)),
            pltpu.SemaphoreType.DMA((slabs, narrow - 1)),
            pltpu.SemaphoreType.DMA((3,)),
            pltpu.SemaphoreType.DMA((3,)),
        ],
        compiler_params=pltpu.CompilerParams(
            collective_id=0, has_side_effects=True, vmem_limit_bytes=24 << 20),
    )(*[pltpu.with_memory_space_constraint(value, pltpu.HBM) for value in (vector, gates)])
    return result.reshape(layout)


def tiled(order, count):
    return count > 1 and count & (count - 1) == 0 and order % (8 * count) == 0


def solution(mesh):
    wide, narrow = mesh.shape["wide"], mesh.shape["narrow"]

    def shards(amplitudes, gates):
        order = amplitudes.shape[4]
        if tiled(order, wide) and tiled(order, narrow) and wide * narrow <= 128:
            return fused(wide, narrow, amplitudes, gates)
        return plain(amplitudes, gates)

    return jax.shard_map(
        shards,
        mesh=mesh,
        in_specs=(P(None, None, "wide", "narrow", None, None), P()),
        out_specs=P(None, None, "wide", "narrow", None, None),
        check_vma=False,
    )
```

```python
import functools

import jax
import jax.numpy as jnp
from jax import lax
from jax.experimental import pallas as pl
from jax.experimental.pallas import tpu as pltpu
from jax.sharding import PartitionSpec as P

precise = lax.Precision.HIGHEST
MESH = pl.DeviceIdType.MESH
F32 = jnp.float32
BF16 = jnp.bfloat16
EARLY_AT = 4
TAIL = 1


def blocks(matrix):
    return jnp.stack([jnp.stack([matrix[0], -matrix[1]]), jnp.stack([matrix[1], matrix[0]])])


def on_rows(vector, matrix):
    return jnp.einsum("cdjk,drkb->crjb", blocks(matrix), vector, precision=precise)


def on_columns(vector, matrix):
    return jnp.einsum("cdjk,drak->craj", blocks(matrix), vector, precision=precise)


def plain(amplitudes, gates):
    layout = amplitudes.shape
    slabs, order = layout[1], layout[4]
    vector = amplitudes.reshape(2, slabs, order, order)
    vector = on_columns(on_rows(vector, gates[0, 0]), gates[0, 1])
    vector = lax.all_to_all(vector.reshape(layout), "wide", split_axis=4, concat_axis=2, tiled=True)
    vector = vector.reshape(2, slabs, order, order)
    vector = on_columns(on_rows(vector, gates[1, 0]), gates[1, 1])
    vector = lax.all_to_all(vector.reshape(layout), "narrow", split_axis=4, concat_axis=3, tiled=True)
    vector = vector.reshape(2, slabs, order, order)
    vector = on_columns(on_rows(vector, gates[2, 0]), gates[2, 1])
    return vector.reshape(layout)


def partner(me, mask, count):
    out, bit = 0, 1
    while bit < count:
        digit = me // bit % 2
        if mask & bit:
            digit = 1 - digit
        out = out + digit * bit
        bit *= 2
    return out


def far_first(count):
    return sorted(range(1, count), key=lambda m: (-bin(m >> 1).count("1"), -m))


def split(value):
    high = value.astype(BF16)
    return high, (value - high.astype(F32)).astype(BF16)


def real_form(matrix):
    re, im = matrix[0], matrix[1]
    return jnp.concatenate(
        [jnp.concatenate([re, -im], axis=1), jnp.concatenate([im, re], axis=1)], axis=0
    )


def kernel(wide, narrow, early, amp, gates, out, x, g, y, yr, z, zr, left, right,
           load_sem, gate_sem, ws_sem, wr_sem, ns_sem, nr_sem, es_sem, er_sem):
    slabs, order = amp.shape[1], amp.shape[2]
    last = slabs - 1
    hw, hn = order // wide, order // narrow
    w, n = lax.axis_index("wide"), lax.axis_index("narrow")
    wide_masks = far_first(wide)
    narrow_masks = far_first(narrow)

    barrier = pltpu.get_barrier_semaphore()
    for mask in wide_masks:
        pl.semaphore_signal(barrier, inc=1, device_id=(partner(w, mask, wide), n), device_id_type=MESH)
    for mask in narrow_masks:
        pl.semaphore_signal(barrier, inc=1, device_id=(w, partner(n, mask, narrow)), device_id_type=MESH)

    def load(c):
        return pltpu.make_async_copy(amp.at[:, c], x.at[:, c], load_sem.at[c])

    def load_gate(t, k):
        return pltpu.make_async_copy(gates.at[t, k], g.at[t, k], gate_sem.at[t, k])

    load_gate(0, 0).start()
    if early:
        load(last).start()
    load(0).start()
    for t in range(3):
        for k in range(2):
            if (t, k) != (0, 0):
                load_gate(t, k).start()
    for c in range(1, last if early else slabs):
        load(c).start()

    def send_wide(c, i):
        there = partner(w, wide_masks[i], wide)
        return pltpu.make_async_remote_copy(
            src_ref=y.at[c, :, pl.ds(pl.multiple_of(there * hw, hw), hw), :],
            dst_ref=yr.at[c, :, pl.ds(pl.multiple_of(w * hw, hw), hw), :],
            send_sem=ws_sem.at[c, i], recv_sem=wr_sem.at[c, i],
            device_id=(there, n), device_id_type=MESH)

    def send_narrow(c, i):
        there = partner(n, narrow_masks[i], narrow)
        return pltpu.make_async_remote_copy(
            src_ref=z.at[c, :, pl.ds(pl.multiple_of(there * hn, hn), hn), :],
            dst_ref=zr.at[c, :, pl.ds(pl.multiple_of(n * hn, hn), hn), :],
            send_sem=ns_sem.at[c, i], recv_sem=nr_sem.at[c, i],
            device_id=(w, there), device_id_type=MESH)

    def send_early():
        return pltpu.make_async_remote_copy(
            src_ref=x.at[:, last], dst_ref=x.at[:, slabs],
            send_sem=es_sem.at[0], recv_sem=er_sem.at[0],
            device_id=(w, partner(n, 3, narrow)), device_id_type=MESH)

    def send_half(k):
        there = partner(n, 1, narrow)
        index = partner(n, 3 * k, narrow)
        return pltpu.make_async_remote_copy(
            src_ref=z.at[last + k, :, pl.ds(pl.multiple_of(there * hn, hn), hn), :],
            dst_ref=zr.at[last, :, pl.ds(pl.multiple_of(index * hn, hn), hn), :],
            send_sem=es_sem.at[1 + k], recv_sem=er_sem.at[1 + k],
            device_id=(w, there), device_id_type=MESH)

    def prepare(t):
        load_gate(t, 0).wait()
        high, low = split(real_form(g[t, 0]))
        left[t] = jnp.concatenate([high, low, high], axis=1)

    def rows(t, value):
        high, low = split(value.reshape(2 * order, order))
        stacked = jnp.concatenate([high, high, low], axis=0)
        return jnp.dot(left[t], stacked, preferred_element_type=F32)

    def columns(value):
        high, low = split(jnp.concatenate([value[:order], value[order:]], axis=1))
        stacked = jnp.concatenate([high, low, high], axis=1)
        return jnp.dot(stacked, right[...], preferred_element_type=F32)

    def first(c, loaded=False):
        if not loaded:
            load(c).wait()
        y[c] = rows(0, x[:, c]).reshape(2, order, order)

    def start_wide(c):
        for i in range(wide - 1):
            send_wide(c, i).start()

    prepare(0)
    first(0)
    if early:
        load(last).wait()
    pl.semaphore_wait(barrier, wide + narrow - 2)
    if early:
        send_early().start()
    start_wide(0)
    prepare(1)

    @pl.loop(1, last if early else slabs)
    def _(c):
        first(c)
        start_wide(c)

    if early:
        first(last, True)
        start_wide(last)

    def second(c, with_columns, with_narrow=True):
        own = pl.ds(pl.multiple_of(w * hw, hw), hw)
        yr[c, :, own, :] = y[c, :, own, :]
        for i in range(wide - 1):
            send_wide(c, i).wait_recv()
        value = rows(1, yr[c])
        if with_columns:
            value = columns(value)
            z[c, 0] = value[:, :order]
            z[c, 1] = value[:, order:]
        else:
            z[c] = value.reshape(2, order, order)
        if not with_narrow:
            return
        for i in range(narrow - 1):
            send_narrow(c, i).start()

    second(0, False)

    for t in range(3):
        load_gate(t, 1).wait()
    product = g[0, 1].reshape(2 * order, order)
    for t in (1, 2):
        product = jnp.dot(real_form(g[t, 1]), product, precision=precise, preferred_element_type=F32)
    re, im = product[:order].T, product[order:].T
    high, low = split(jnp.concatenate(
        [jnp.concatenate([re, im], axis=1), jnp.concatenate([-im, re], axis=1)], axis=0))
    right[...] = jnp.concatenate([high, high, low], axis=0)
    prepare(2)

    if early:
        @pl.loop(1, EARLY_AT)
        def _(c):
            second(c, True)

        send_early().wait_recv()
        first(slabs, True)
        start_wide(slabs)

        @pl.loop(EARLY_AT, last - TAIL)
        def _(c):
            second(c, True)

        @pl.loop(last, slabs + 1)
        def _(c):
            second(c, False, False)

        for k in range(2):
            send_half(k).start()
            index = partner(n, 3 * k, narrow)
            rows_to = pl.ds(pl.multiple_of(index * hn, hn), hn)
            rows_from = pl.ds(pl.multiple_of(n * hn, hn), hn)
            zr[last, :, rows_to, :] = z[last + k, :, rows_from, :]

        @pl.loop(last - TAIL, last)
        def _(c):
            second(c, True)
    else:
        @pl.loop(1, slabs)
        def _(c):
            second(c, True)

    def third(c, with_columns, exchanged=False):
        if not exchanged:
            own = pl.ds(pl.multiple_of(n * hn, hn), hn)
            zr[c, :, own, :] = z[c, :, own, :]
            for i in range(narrow - 1):
                send_narrow(c, i).wait_recv()
        value = rows(2, zr[c])
        if with_columns:
            value = columns(value)
            out[0, c] = value[:, :order]
            out[1, c] = value[:, order:]
        else:
            out[0, c] = value[:order]
            out[1, c] = value[order:]

    third(0, True)
    if early:
        @pl.loop(1, last - TAIL)
        def _(c):
            third(c, False)

        for k in range(2):
            send_half(k).wait_recv()
        third(last, True, True)

        @pl.loop(last - TAIL, last)
        def _(c):
            third(c, False)
    else:
        @pl.loop(1, slabs)
        def _(c):
            third(c, False)

    @pl.loop(0, slabs + 1 if early else slabs)
    def _(c):
        for i in range(wide - 1):
            send_wide(c, i).wait_send()

    @pl.loop(0, last if early else slabs)
    def _(c):
        for i in range(narrow - 1):
            send_narrow(c, i).wait_send()

    if early:
        send_early().wait_send()
        for k in range(2):
            send_half(k).wait_send()


def fused(wide, narrow, amplitudes, gates):
    layout = amplitudes.shape
    slabs, order = layout[1], layout[4]
    vector = amplitudes.reshape(2, slabs, order, order)
    early = narrow == 4 and slabs > EARLY_AT + TAIL
    slots = slabs + early
    slab_buffer = pltpu.VMEM((slots, 2, order, order), F32)
    result = pl.pallas_call(
        functools.partial(kernel, wide, narrow, early),
        out_shape=jax.ShapeDtypeStruct(vector.shape, F32),
        in_specs=[pl.BlockSpec(memory_space=pl.ANY)] * 2,
        out_specs=pl.BlockSpec(memory_space=pltpu.VMEM),
        scratch_shapes=[
            pltpu.VMEM((2, slots, order, order), F32),
            pltpu.VMEM(gates.shape, F32),
            slab_buffer, slab_buffer, slab_buffer, slab_buffer,
            pltpu.VMEM((3, 2 * order, 6 * order), BF16),
            pltpu.VMEM((6 * order, 2 * order), BF16),
            pltpu.SemaphoreType.DMA((slabs,)),
            pltpu.SemaphoreType.DMA((3, 2)),
            pltpu.SemaphoreType.DMA((slots, wide - 1)),
            pltpu.SemaphoreType.DMA((slots, wide - 1)),
            pltpu.SemaphoreType.DMA((slabs, narrow - 1)),
            pltpu.SemaphoreType.DMA((slabs, narrow - 1)),
            pltpu.SemaphoreType.DMA((3,)),
            pltpu.SemaphoreType.DMA((3,)),
        ],
        compiler_params=pltpu.CompilerParams(
            collective_id=0, has_side_effects=True, vmem_limit_bytes=24 << 20),
    )(*[pltpu.with_memory_space_constraint(value, pltpu.HBM) for value in (vector, gates)])
    return result.reshape(layout)


def tiled(order, count):
    return count > 1 and count & (count - 1) == 0 and order % (8 * count) == 0


def solution(mesh):
    wide, narrow = mesh.shape["wide"], mesh.shape["narrow"]

    def shards(amplitudes, gates):
        order = amplitudes.shape[4]
        if tiled(order, wide) and tiled(order, narrow) and wide * narrow <= 128:
            return fused(wide, narrow, amplitudes, gates)
        return plain(amplitudes, gates)

    return jax.shard_map(
        shards,
        mesh=mesh,
        in_specs=(P(None, None, "wide", "narrow", None, None), P()),
        out_specs=P(None, None, "wide", "narrow", None, None),
        check_vma=False,
    )
```

```python
import functools

import jax
import jax.numpy as jnp
from jax import lax
from jax.experimental import pallas as pl
from jax.experimental.pallas import tpu as pltpu
from jax.sharding import PartitionSpec as P

precise = lax.Precision.HIGHEST
MESH = pl.DeviceIdType.MESH
F32 = jnp.float32
BF16 = jnp.bfloat16
EARLY_AT = 4
TAIL = 1


def blocks(matrix):
    return jnp.stack([jnp.stack([matrix[0], -matrix[1]]), jnp.stack([matrix[1], matrix[0]])])


def on_rows(vector, matrix):
    return jnp.einsum("cdjk,drkb->crjb", blocks(matrix), vector, precision=precise)


def on_columns(vector, matrix):
    return jnp.einsum("cdjk,drak->craj", blocks(matrix), vector, precision=precise)


def plain(amplitudes, gates):
    layout = amplitudes.shape
    slabs, order = layout[1], layout[4]
    vector = amplitudes.reshape(2, slabs, order, order)
    vector = on_columns(on_rows(vector, gates[0, 0]), gates[0, 1])
    vector = lax.all_to_all(vector.reshape(layout), "wide", split_axis=4, concat_axis=2, tiled=True)
    vector = vector.reshape(2, slabs, order, order)
    vector = on_columns(on_rows(vector, gates[1, 0]), gates[1, 1])
    vector = lax.all_to_all(vector.reshape(layout), "narrow", split_axis=4, concat_axis=3, tiled=True)
    vector = vector.reshape(2, slabs, order, order)
    vector = on_columns(on_rows(vector, gates[2, 0]), gates[2, 1])
    return vector.reshape(layout)


def partner(me, mask, count):
    out, bit = 0, 1
    while bit < count:
        digit = me // bit % 2
        if mask & bit:
            digit = 1 - digit
        out = out + digit * bit
        bit *= 2
    return out


def far_first(count):
    return sorted(range(1, count), key=lambda m: (-bin(m >> 1).count("1"), -m))


def split(value):
    high = value.astype(BF16)
    return high, (value - high.astype(F32)).astype(BF16)


def real_form(matrix):
    re, im = matrix[0], matrix[1]
    return jnp.concatenate(
        [jnp.concatenate([re, -im], axis=1), jnp.concatenate([im, re], axis=1)], axis=0
    )


def kernel(wide, narrow, early, amp, gates, out, x, g, y, yr, z, zr, left, right,
           load_sem, gate_sem, ws_sem, wr_sem, ns_sem, nr_sem, es_sem, er_sem):
    slabs, order = amp.shape[1], amp.shape[2]
    last = slabs - 1
    hw, hn = order // wide, order // narrow
    w, n = lax.axis_index("wide"), lax.axis_index("narrow")
    wide_masks = far_first(wide)
    narrow_masks = list(range(1, narrow))

    barrier = pltpu.get_barrier_semaphore()
    for mask in wide_masks:
        pl.semaphore_signal(barrier, inc=1, device_id=(partner(w, mask, wide), n), device_id_type=MESH)
    for mask in narrow_masks:
        pl.semaphore_signal(barrier, inc=1, device_id=(w, partner(n, mask, narrow)), device_id_type=MESH)

    def load(c):
        return pltpu.make_async_copy(amp.at[:, c], x.at[:, c], load_sem.at[c])

    def load_gate(t, k):
        return pltpu.make_async_copy(gates.at[t, k], g.at[t, k], gate_sem.at[t, k])

    load_gate(0, 0).start()
    if early:
        load(last).start()
    load(0).start()
    for t in range(3):
        for k in range(2):
            if (t, k) != (0, 0):
                load_gate(t, k).start()
    for c in range(1, last if early else slabs):
        load(c).start()

    def send_wide(c, i):
        there = partner(w, wide_masks[i], wide)
        return pltpu.make_async_remote_copy(
            src_ref=y.at[c, :, pl.ds(pl.multiple_of(there * hw, hw), hw), :],
            dst_ref=yr.at[c, :, pl.ds(pl.multiple_of(w * hw, hw), hw), :],
            send_sem=ws_sem.at[c, i], recv_sem=wr_sem.at[c, i],
            device_id=(there, n), device_id_type=MESH)

    def send_narrow(c, i):
        there = partner(n, narrow_masks[i], narrow)
        return pltpu.make_async_remote_copy(
            src_ref=z.at[c, :, pl.ds(pl.multiple_of(there * hn, hn), hn), :],
            dst_ref=zr.at[c, :, pl.ds(pl.multiple_of(n * hn, hn), hn), :],
            send_sem=ns_sem.at[c, i], recv_sem=nr_sem.at[c, i],
            device_id=(w, there), device_id_type=MESH)

    def send_early():
        return pltpu.make_async_remote_copy(
            src_ref=x.at[:, last], dst_ref=x.at[:, slabs],
            send_sem=es_sem.at[0], recv_sem=er_sem.at[0],
            device_id=(w, partner(n, 3, narrow)), device_id_type=MESH)

    def send_half(k):
        there = partner(n, 1, narrow)
        index = partner(n, 3 * k, narrow)
        return pltpu.make_async_remote_copy(
            src_ref=z.at[last + k, :, pl.ds(pl.multiple_of(there * hn, hn), hn), :],
            dst_ref=zr.at[last, :, pl.ds(pl.multiple_of(index * hn, hn), hn), :],
            send_sem=es_sem.at[1 + k], recv_sem=er_sem.at[1 + k],
            device_id=(w, there), device_id_type=MESH)

    def prepare(t):
        load_gate(t, 0).wait()
        high, low = split(real_form(g[t, 0]))
        left[t] = jnp.concatenate([high, low, high], axis=1)

    def rows(t, value):
        high, low = split(value.reshape(2 * order, order))
        stacked = jnp.concatenate([high, high, low], axis=0)
        return jnp.dot(left[t], stacked, preferred_element_type=F32)

    def columns(value):
        high, low = split(jnp.concatenate([value[:order], value[order:]], axis=1))
        stacked = jnp.concatenate([high, low, high], axis=1)
        return jnp.dot(stacked, right[...], preferred_element_type=F32)

    def first(c, loaded=False):
        if not loaded:
            load(c).wait()
        y[c] = rows(0, x[:, c]).reshape(2, order, order)

    def start_wide(c):
        for i in range(wide - 1):
            send_wide(c, i).start()

    prepare(0)
    first(0)
    if early:
        load(last).wait()
    pl.semaphore_wait(barrier, wide + narrow - 2)
    if early:
        send_early().start()
    start_wide(0)
    prepare(1)

    @pl.loop(1, last if early else slabs)
    def _(c):
        first(c)
        start_wide(c)

    if early:
        first(last, True)
        start_wide(last)

    def second(c, with_columns, with_narrow=True):
        own = pl.ds(pl.multiple_of(w * hw, hw), hw)
        yr[c, :, own, :] = y[c, :, own, :]
        for i in range(wide - 1):
            send_wide(c, i).wait_recv()
        value = rows(1, yr[c])
        if with_columns:
            value = columns(value)
            z[c, 0] = value[:, :order]
            z[c, 1] = value[:, order:]
        else:
            z[c] = value.reshape(2, order, order)
        if not with_narrow:
            return
        for i in range(narrow - 1):
            send_narrow(c, i).start()

    second(0, False)

    for t in range(3):
        load_gate(t, 1).wait()
    product = g[0, 1].reshape(2 * order, order)
    for t in (1, 2):
        product = jnp.dot(real_form(g[t, 1]), product, precision=precise, preferred_element_type=F32)
    re, im = product[:order].T, product[order:].T
    high, low = split(jnp.concatenate(
        [jnp.concatenate([re, im], axis=1), jnp.concatenate([-im, re], axis=1)], axis=0))
    right[...] = jnp.concatenate([high, high, low], axis=0)
    prepare(2)

    if early:
        @pl.loop(1, EARLY_AT)
        def _(c):
            second(c, True)

        send_early().wait_recv()
        first(slabs, True)
        start_wide(slabs)

        @pl.loop(EARLY_AT, last - TAIL)
        def _(c):
            second(c, True)

        @pl.loop(last, slabs + 1)
        def _(c):
            second(c, False, False)

        for k in range(2):
            send_half(k).start()
            index = partner(n, 3 * k, narrow)
            rows_to = pl.ds(pl.multiple_of(index * hn, hn), hn)
            rows_from = pl.ds(pl.multiple_of(n * hn, hn), hn)
            zr[last, :, rows_to, :] = z[last + k, :, rows_from, :]

        @pl.loop(last - TAIL, last)
        def _(c):
            second(c, True)
    else:
        @pl.loop(1, slabs)
        def _(c):
            second(c, True)

    def third(c, with_columns, exchanged=False):
        if not exchanged:
            own = pl.ds(pl.multiple_of(n * hn, hn), hn)
            zr[c, :, own, :] = z[c, :, own, :]
            for i in range(narrow - 1):
                send_narrow(c, i).wait_recv()
        value = rows(2, zr[c])
        if with_columns:
            value = columns(value)
            out[0, c] = value[:, :order]
            out[1, c] = value[:, order:]
        else:
            out[0, c] = value[:order]
            out[1, c] = value[order:]

    third(0, True)
    if early:
        @pl.loop(1, last - TAIL)
        def _(c):
            third(c, False)

        for k in range(2):
            send_half(k).wait_recv()
        third(last, True, True)

        @pl.loop(last - TAIL, last)
        def _(c):
            third(c, False)
    else:
        @pl.loop(1, slabs)
        def _(c):
            third(c, False)

    @pl.loop(0, slabs + 1 if early else slabs)
    def _(c):
        for i in range(wide - 1):
            send_wide(c, i).wait_send()

    @pl.loop(0, last if early else slabs)
    def _(c):
        for i in range(narrow - 1):
            send_narrow(c, i).wait_send()

    if early:
        send_early().wait_send()
        for k in range(2):
            send_half(k).wait_send()


def fused(wide, narrow, amplitudes, gates):
    layout = amplitudes.shape
    slabs, order = layout[1], layout[4]
    vector = amplitudes.reshape(2, slabs, order, order)
    early = narrow == 4 and slabs > EARLY_AT + TAIL
    slots = slabs + early
    slab_buffer = pltpu.VMEM((slots, 2, order, order), F32)
    result = pl.pallas_call(
        functools.partial(kernel, wide, narrow, early),
        out_shape=jax.ShapeDtypeStruct(vector.shape, F32),
        in_specs=[pl.BlockSpec(memory_space=pl.ANY)] * 2,
        out_specs=pl.BlockSpec(memory_space=pltpu.VMEM),
        scratch_shapes=[
            pltpu.VMEM((2, slots, order, order), F32),
            pltpu.VMEM(gates.shape, F32),
            slab_buffer, slab_buffer, slab_buffer, slab_buffer,
            pltpu.VMEM((3, 2 * order, 6 * order), BF16),
            pltpu.VMEM((6 * order, 2 * order), BF16),
            pltpu.SemaphoreType.DMA((slabs,)),
            pltpu.SemaphoreType.DMA((3, 2)),
            pltpu.SemaphoreType.DMA((slots, wide - 1)),
            pltpu.SemaphoreType.DMA((slots, wide - 1)),
            pltpu.SemaphoreType.DMA((slabs, narrow - 1)),
            pltpu.SemaphoreType.DMA((slabs, narrow - 1)),
            pltpu.SemaphoreType.DMA((3,)),
            pltpu.SemaphoreType.DMA((3,)),
        ],
        compiler_params=pltpu.CompilerParams(
            collective_id=0, has_side_effects=True, vmem_limit_bytes=24 << 20),
    )(*[pltpu.with_memory_space_constraint(value, pltpu.HBM) for value in (vector, gates)])
    return result.reshape(layout)


def tiled(order, count):
    return count > 1 and count & (count - 1) == 0 and order % (8 * count) == 0


def solution(mesh):
    wide, narrow = mesh.shape["wide"], mesh.shape["narrow"]

    def shards(amplitudes, gates):
        order = amplitudes.shape[4]
        if tiled(order, wide) and tiled(order, narrow) and wide * narrow <= 128:
            return fused(wide, narrow, amplitudes, gates)
        return plain(amplitudes, gates)

    return jax.shard_map(
        shards,
        mesh=mesh,
        in_specs=(P(None, None, "wide", "narrow", None, None), P()),
        out_specs=P(None, None, "wide", "narrow", None, None),
        check_vma=False,
    )
```
